32 devices in a mesh: rep: 16 (over z, x, core), exp: 2 (over y).
Axes of the slice: x: 2, y: 2, z: 4, core: 2. Of those that a mesh axis runs over, the one named last changes fastest.
Arguments:
- hidden_states: bfloat16 [8192, 384], P(('rep', 'exp')), may hold values from -6 to 6
- expert_ids: int32 [8192, 2], P(('rep', 'exp')), may hold values from 0 to 7, all different within a row; in each aligned block of 256 rows (0 to 255, 256 to 511, ...) at most 96 rows name the same one
- router_weight: bfloat16 [384, 8], replicated, may hold values from -0.3125 to 0.3125
- up_weight: bfloat16 [8, 384, 2048], P('exp'), may hold values from -0.3125 to 0.3125
- down_weight: bfloat16 [8, 2048, 384], P('exp'), may hold values from -0.125 to 0.125
- projection: bfloat16 [384, 128], replicated, may hold values from -0.3125 to 0.3125
- teacher_scores: float32 [32, 32, 224], P(('rep', 'exp')), may hold values from -8 to 8
- query_lengths: int32 [32], P(('rep', 'exp')), may hold values from 8 to 32
- passage_lengths: int32 [32], P(('rep', 'exp')), may hold values from 56 to 224
Outputs:
- input_grad: bfloat16 [8192, 384], P(('rep', 'exp'))
- down_grad: float32 [8, 2048, 384], P('exp', 'rep')
- pair_kl: float32 [32], P(('rep', 'exp'))
The draws below stay inside these ranges and needn't reach their ends.
Inputs may be any that keep to these rules, and one draw needn't show every extreme that they name: `expert_ids`: each row names 2 different experts. In the 256 rows of one device no expert is named more than 96 times, and in every draw some device names some expert exactly 96 times.
All inputs are finite; a program needn't handle non-finite values.
Results may differ from the reference program's by a relative error of at most 0.0086.
Values may be sent and summed in bfloat16 or wider, within the bound.
A program may use at most 64 MiB of HBM per device.

```python
import math
import jax
import jax.numpy as jnp
import numpy as np
from jax import lax

D = 384
FF = 2048
E = 8
TOP = 2
VEC = 128
LQ = 32
LP = 224
SEQ = 256
TOK_DEV = 256
CAP = 96
PAIRS = 32
TOKENS = 8192


def place_ends(entries, stream_key, low, high):
    index_at = [jax.random.randint(jax.random.fold_in(stream_key, axis), (), 0, length) for axis, length in enumerate(entries.shape)]
    widest = entries.shape.index(max(entries.shape))
    neighbour = index_at[:widest] + [(index_at[widest] + 1) % entries.shape[widest]] + index_at[widest + 1:]
    return entries.at[tuple(index_at)].set(low).at[tuple(neighbour)].set(high)


def steps_of(key, extent, split, smallest, high):
    def one(position, blocks):
        draws = jax.random.uniform(jax.random.fold_in(jax.random.fold_in(key, 6), position), (blocks,), jnp.float32, smallest / len(split), high / len(split))
        return jnp.repeat(jnp.exp(draws), extent[position] // blocks).reshape((-1,) + (1,) * (len(extent) - position - 1))

    loudness = one(*split[0])
    for cut in split[1:]:
        loudness = loudness * one(*cut)
    return loudness


def assign_block(stream_key, own, number, rows, number_of, top, reach, skew):
    order = jax.random.permutation(stream_key, number_of)
    crowded, ordinary = shares(number_of, rows * top, reach, skew, True), shares(number_of, rows * top, reach, skew, False)
    places = jnp.arange(number_of)

    def named(lengths, offset_by):
        used = int((lengths > 0).sum())
        fixed = max(1, used // 4)
        shifted = fixed + (places - fixed + offset_by * (used - fixed)) % max(1, number_of - fixed)
        return jnp.zeros((number_of,), jnp.int32).at[order[jnp.where(places < fixed, places, shifted)]].set(jnp.asarray(lengths, jnp.int32))

    lengths = jnp.where(number % 4 == 0, named(crowded, number // 4), named(ordinary, number - number // 4 - 1))
    mixed = jax.random.permutation(jax.random.fold_in(own, 3), number_of)
    source_of, taker = mixed[0:number_of // 2 * 2:2], mixed[1:number_of // 2 * 2:2]
    margin = jnp.minimum(lengths[source_of] - 1, reach - lengths[taker]) // 2
    margin = jnp.where((source_of == order[0]) | (taker == order[0]) | (lengths[taker] == 0), 0, jnp.maximum(margin, 0))
    shifted = jax.random.randint(jax.random.fold_in(own, 4), (number_of // 2,), 0, 1 << 20) % (margin + 1)
    lengths = lengths.at[source_of].add(-shifted).at[taker].add(shifted)
    labels = jnp.searchsorted(jnp.cumsum(lengths), jnp.arange(rows * top), side="right").astype(jnp.int32)
    grid = labels.reshape(top, rows).T
    grid = grid[jax.random.permutation(jax.random.fold_in(own, 1), rows)]
    offset_by = jax.random.randint(jax.random.fold_in(own, 2), (rows, 1), 0, top)
    return jnp.take_along_axis(grid, (jnp.arange(top)[None, :] + offset_by) % top, axis=1)


def shares(amount, total, limit, slope, full):
    loads = [(1 << 20) // math.isqrt(standing ** slope) + 1 for standing in range(1, amount + 1)]
    largest = limit if full else min(limit, max(-(-total // amount), total * loads[0] // sum(loads)))
    least = 1 if total - largest >= amount - 1 else 0
    holding, spare = [largest] + [least] * (amount - 1), total - largest - least * (amount - 1)
    while spare > 0:
        candidates = [i for i in range(1, amount) if holding[i] < largest] or [i for i in range(1, amount) if holding[i] < limit]
        pool, budget = sum([loads[i] for i in candidates]), spare
        for i in candidates:
            addition = min(limit - holding[i], max(1, budget * loads[i] // pool), spare)
            holding[i] = holding[i] + addition
            spare = spare - addition
    return np.array(holding)


def bell_draw(rng, extent, deviation, reach, cuts=(), kind=jnp.bfloat16):
    result = deviation * jax.random.normal(rng, extent, jnp.float32)
    if cuts:
        result = result * steps_of(rng, extent, cuts, -0.22, 0.18)
    return jnp.clip(result, -reach, reach).astype(kind)


def setup_inputs(seed: int = 0) -> dict:
    arg_keys = jax.random.split(jax.random.key(seed), 10)
    hidden_states = bell_draw(arg_keys[0], (TOKENS, D), 1.0, 6.0, ((0, 32),))
    expert_ids_keys = jax.random.split(jax.random.fold_in(arg_keys[1], 1), TOKENS // TOK_DEV)
    expert_ids_turns = jax.random.permutation(jax.random.fold_in(arg_keys[1], 3), TOKENS // TOK_DEV)
    expert_ids = jax.vmap(lambda own, number: assign_block(jax.random.fold_in(arg_keys[1], 2), own, number, TOK_DEV, E, TOP, CAP, 2))(expert_ids_keys, expert_ids_turns).reshape((TOKENS, TOP))
    router_weight = bell_draw(arg_keys[2], (D, E), D ** -0.5, 0.3125)
    up_weight = bell_draw(arg_keys[3], (E, D, FF), D ** -0.5, 0.3125, ((0, 2),))
    down_weight = bell_draw(arg_keys[4], (E, FF, D), FF ** -0.5, 0.125, ((0, 2),))
    projection = bell_draw(arg_keys[5], (D, VEC), D ** -0.5, 0.3125)
    teacher_scores = jnp.clip(jax.random.uniform(arg_keys[6], (PAIRS, LQ, LP), jnp.float32, -8.0, 8.0) * steps_of(arg_keys[6], (PAIRS, LQ, LP), ((0, 32),), -0.4, 0.0), -8.0, 8.0)
    query_lengths = place_ends(jax.random.randint(arg_keys[7], (PAIRS,), LQ // 4, LQ + 1), jax.random.fold_in(arg_keys[7], 1), LQ // 4, LQ).astype(jnp.int32)
    passage_lengths = place_ends(jax.random.randint(arg_keys[8], (PAIRS,), LP // 4, LP + 1), jax.random.fold_in(arg_keys[8], 1), LP // 4, LP).astype(jnp.int32)
    return {"hidden_states": hidden_states, "expert_ids": expert_ids, "router_weight": router_weight, "up_weight": up_weight, "down_weight": down_weight, "projection": projection, "teacher_scores": teacher_scores, "query_lengths": query_lengths, "passage_lengths": passage_lengths}


score_scale = 20.0
norm_eps = 1e-06
sqrt_half = 0.7071067811865476
density_scale = 0.3989422804014327

def gelu_value(preact):
    return 0.5 * preact * (1.0 + lax.erf(preact * sqrt_half))

def gelu_slope(preact):
    return 0.5 * (1.0 + lax.erf(preact * sqrt_half)) + preact * jnp.exp(-0.5 * preact * preact) * density_scale

def distill(vectors, teacher_scores, query_lengths, passage_lengths):
    queries = vectors[:, :LQ]
    passages = vectors[:, LQ:]
    scores = score_scale * jnp.einsum('pqv,pkv->pqk', queries, passages, precision=lax.Precision.HIGHEST)
    query_mask = (jnp.arange(LQ, dtype=jnp.int32)[None, :] < query_lengths[:, None]).astype(jnp.float32)
    passage_mask = (jnp.arange(LP, dtype=jnp.int32)[None, :] < passage_lengths[:, None]).astype(jnp.float32)
    student_exp = jnp.exp(scores) * passage_mask[:, None, :]
    student_total = lax.optimization_barrier(jnp.sum(student_exp, axis=-1, keepdims=True))
    student = student_exp / student_total
    log_student = scores - jnp.log(student_total)
    teacher_exp = jnp.exp(teacher_scores) * passage_mask[:, None, :]
    teacher_total = lax.optimization_barrier(jnp.sum(teacher_exp, axis=-1, keepdims=True))
    teacher = teacher_exp / teacher_total
    log_teacher = teacher_scores - jnp.log(teacher_total)
    per_query = lax.optimization_barrier(jnp.sum(teacher * (log_teacher - log_student), axis=-1))
    pair_kl = lax.optimization_barrier(jnp.sum(per_query * query_mask, axis=-1))
    score_grad = (student - teacher) * query_mask[:, :, None]
    query_grad = score_scale * jnp.einsum('pqk,pkv->pqv', score_grad, passages, precision=lax.Precision.HIGHEST)
    passage_grad = score_scale * jnp.einsum('pqk,pqv->pkv', score_grad, queries, precision=lax.Precision.HIGHEST)
    return (pair_kl, jnp.concatenate([query_grad, passage_grad], axis=1))

def route_targets(block_ids):
    onehot = (block_ids[..., None] == jnp.arange(E, dtype=jnp.int32)).astype(jnp.int32)
    earlier = jnp.cumsum(onehot, axis=1) - onehot
    slots = lax.optimization_barrier(jnp.sum(earlier * onehot, axis=-1))
    return (block_ids * CAP + slots).astype(jnp.int32)

def group_blocks(expert_rows):
    groups = expert_rows.shape[0]
    per_block = 16 if groups % 16 == 0 else 1
    return expert_rows.reshape(groups // per_block, per_block * CAP, D)

def expert_forward(operands):
    weight_up, weight_down, expert_rows = operands

    def one_block(block_rows):
        preact = jnp.dot(block_rows, weight_up, preferred_element_type=jnp.float32)
        hidden = gelu_value(preact).astype(jnp.bfloat16)
        return jnp.dot(hidden, weight_down, preferred_element_type=jnp.float32).astype(jnp.bfloat16)
    outputs = lax.map(one_block, group_blocks(expert_rows))
    return outputs.reshape(expert_rows.shape)

def expert_backward(operands):
    weight_up, weight_down, expert_rows, expert_grads = operands

    def one_block(total, pieces):
        block_rows, block_grads = pieces
        preact = jnp.dot(block_rows, weight_up, preferred_element_type=jnp.float32)
        hidden = gelu_value(preact).astype(jnp.bfloat16)
        total = total + jnp.dot(hidden.T, block_grads, preferred_element_type=jnp.float32)
        hidden_grad = jnp.dot(block_grads, weight_down.T, preferred_element_type=jnp.float32)
        pre_grad = (hidden_grad * gelu_slope(preact)).astype(jnp.bfloat16)
        row_grad = jnp.dot(pre_grad, weight_up.T, preferred_element_type=jnp.float32).astype(jnp.bfloat16)
        return (total, row_grad)
    initial = jnp.zeros((FF, D), jnp.float32)
    total, row_grads = lax.scan(one_block, initial, (group_blocks(expert_rows), group_blocks(expert_grads)))
    return (total, row_grads.reshape(expert_rows.shape))

def reference(hidden_states, expert_ids, router_weight, up_weight, down_weight, projection, teacher_scores, query_lengths, passage_lengths):
    groups = TOKENS // TOK_DEV
    route_count = TOK_DEV * TOP
    logits = jnp.dot(hidden_states, router_weight, preferred_element_type=jnp.float32)
    choose = (expert_ids[..., None] == jnp.arange(E, dtype=jnp.int32)).astype(jnp.float32)
    picked = lax.optimization_barrier(jnp.sum(logits[:, None, :] * choose, axis=-1))
    first_gate = jax.nn.sigmoid(picked[:, 0] - picked[:, 1])
    gate_values = jnp.stack([first_gate, 1.0 - first_gate], axis=1)
    targets = route_targets(expert_ids.reshape(groups, route_count))
    group_index = jnp.arange(groups, dtype=jnp.int32)[:, None]
    routed = jnp.repeat(hidden_states, TOP, axis=0).reshape(groups, route_count, D)
    buffers = jnp.zeros((groups, E * CAP, D), hidden_states.dtype).at[group_index, targets].set(routed)
    by_expert = buffers.reshape(groups, E, CAP, D).transpose(1, 0, 2, 3)
    outputs = lax.map(expert_forward, (up_weight, down_weight, by_expert))
    outputs_flat = outputs.transpose(1, 0, 2, 3).reshape(groups, E * CAP, D)
    picked_out = jnp.take_along_axis(outputs_flat, targets[..., None], axis=1).reshape(TOKENS, TOP, D)
    mixed_rows = (hidden_states.astype(jnp.float32) + lax.optimization_barrier(jnp.sum(gate_values[:, :, None] * picked_out.astype(jnp.float32), axis=1))).astype(jnp.bfloat16)
    projected = jnp.dot(mixed_rows, projection, preferred_element_type=jnp.float32)
    vec_norm = jnp.sqrt(lax.optimization_barrier(jnp.sum(projected * projected, axis=-1, keepdims=True)) + norm_eps)
    vectors = projected / vec_norm
    pair_kl, vector_grad = distill(vectors.reshape(PAIRS, SEQ, VEC), teacher_scores, query_lengths, passage_lengths)
    vector_grad = vector_grad.reshape(TOKENS, VEC)
    radial = lax.optimization_barrier(jnp.sum(vectors * vector_grad, axis=-1, keepdims=True))
    projected_grad = ((vector_grad - vectors * radial) / vec_norm).astype(jnp.bfloat16)
    mixed_grad = jnp.dot(projected_grad, projection.T, preferred_element_type=jnp.float32)
    out_grad = (gate_values[:, :, None] * mixed_grad[:, None, :]).astype(jnp.bfloat16)
    gate_grad = lax.optimization_barrier(jnp.sum(mixed_grad[:, None, :] * picked_out.astype(jnp.float32), axis=-1))
    spread = (gate_grad[:, 0] - gate_grad[:, 1]) * gate_values[:, 0] * gate_values[:, 1]
    logit_grad = spread[:, None] * (choose[:, 0] - choose[:, 1])
    router_part = jnp.dot(logit_grad, router_weight.astype(jnp.float32).T, precision=lax.Precision.HIGHEST)
    grad_buffers = jnp.zeros((groups, E * CAP, D), out_grad.dtype).at[group_index, targets].set(out_grad.reshape(groups, route_count, D))
    grad_by_expert = grad_buffers.reshape(groups, E, CAP, D).transpose(1, 0, 2, 3)
    down_grad, returned = lax.map(expert_backward, (up_weight, down_weight, by_expert, grad_by_expert))
    returned_flat = returned.transpose(1, 0, 2, 3).reshape(groups, E * CAP, D)
    route_grad = jnp.take_along_axis(returned_flat, targets[..., None], axis=1).reshape(TOKENS, TOP, D)
    input_grad = (mixed_grad + lax.optimization_barrier(jnp.sum(route_grad.astype(jnp.float32), axis=1)) + router_part).astype(jnp.bfloat16)
    return (input_grad, down_grad, pair_kl)
```

```python
import jax
import jax.numpy as jnp
from jax import lax
from jax.sharding import PartitionSpec as P

E = 8
LQ = 32
LP = 224
CAP = 96


score_scale = 20.0
norm_eps = 1e-06
sqrt_half = 0.7071067811865476
density_scale = 0.3989422804014327


def gelu_value(preact):
    return 0.5 * preact * (1.0 + lax.erf(preact * sqrt_half))


def gelu_slope(preact):
    return (
        0.5 * (1.0 + lax.erf(preact * sqrt_half))
        + preact * jnp.exp(-0.5 * preact * preact) * density_scale
    )


def distill(vectors, teacher_scores, query_lengths, passage_lengths):
    queries = vectors[:, :LQ]
    passages = vectors[:, LQ:]
    scores = score_scale * jnp.einsum(
        "pqv,pkv->pqk", queries, passages, precision=lax.Precision.HIGHEST
    )
    query_mask = (jnp.arange(LQ, dtype=jnp.int32)[None, :] < query_lengths[:, None]).astype(
        jnp.float32
    )
    passage_mask = (jnp.arange(LP, dtype=jnp.int32)[None, :] < passage_lengths[:, None]).astype(
        jnp.float32
    )
    student_exp = jnp.exp(scores) * passage_mask[:, None, :]
    student_total = jnp.sum(student_exp, axis=-1, keepdims=True)
    student = student_exp / student_total
    log_student = scores - jnp.log(student_total)
    teacher_exp = jnp.exp(teacher_scores) * passage_mask[:, None, :]
    teacher_total = jnp.sum(teacher_exp, axis=-1, keepdims=True)
    teacher = teacher_exp / teacher_total
    log_teacher = teacher_scores - jnp.log(teacher_total)
    per_query = jnp.sum(teacher * (log_teacher - log_student), axis=-1)
    pair_kl = jnp.sum(per_query * query_mask, axis=-1)
    score_grad = (student - teacher) * query_mask[:, :, None]
    query_grad = score_scale * jnp.einsum(
        "pqk,pkv->pqv", score_grad, passages, precision=lax.Precision.HIGHEST
    )
    passage_grad = score_scale * jnp.einsum(
        "pqk,pqv->pkv", score_grad, queries, precision=lax.Precision.HIGHEST
    )
    return (pair_kl, jnp.concatenate([query_grad, passage_grad], axis=1))


def fetch(block, shift):
    size = lax.axis_size("exp")
    return lax.ppermute(block, "exp", [(i, (i - shift) % size) for i in range(size)])


def give_back(block, shift):
    size = lax.axis_size("exp")
    return lax.ppermute(block, "exp", [(i, (i + shift) % size) for i in range(size)])


def spread_out(block):
    size = lax.axis_size("exp")
    return jnp.stack([block] + [fetch(block, shift) for shift in range(1, size)])


def bring_home(parts):
    total = parts[0]
    for shift in range(1, parts.shape[0]):
        total = total + give_back(parts[shift].astype(jnp.bfloat16), shift).astype(jnp.float32)
    return total


def scatter_sum(terms):
    return lax.psum_scatter(
        terms.astype(jnp.bfloat16), "rep", scatter_dimension=1, tiled=True
    ).astype(jnp.float32)


def local(
    hidden_states,
    expert_ids,
    router_weight,
    up_weight,
    down_weight,
    projection,
    teacher_scores,
    query_lengths,
    passage_lengths,
):
    tok_rows, width = hidden_states.shape
    here = up_weight.shape[0]
    first = lax.axis_index("exp") * here
    rows = spread_out(hidden_states)
    ids = spread_out(expert_ids.T)
    blocks = rows.shape[0]
    names = jnp.arange(E, dtype=jnp.int32)[None, :, None]
    is_first = (ids[:, :1] == names).astype(jnp.float32)
    is_second = (ids[:, 1:] == names).astype(jnp.float32)
    logits = jnp.einsum("de,ntd->net", router_weight, rows, preferred_element_type=jnp.float32)
    side = is_first - is_second
    first_gate = jax.nn.sigmoid(jnp.sum(logits * side, axis=1, keepdims=True))
    second_gate = 1.0 - first_gate
    named = is_first + is_second
    before = jnp.arange(tok_rows)[:, None] < jnp.arange(tok_rows)[None, :]
    slots = jnp.einsum(
        "net,tu->neu",
        named.astype(jnp.bfloat16),
        before.astype(jnp.bfloat16),
        preferred_element_type=jnp.float32,
    ).astype(jnp.int32)
    slots = jnp.where(named > 0, slots, -1)
    mine = lambda value: lax.dynamic_slice_in_dim(value, first, here, axis=1)
    slots_here = mine(slots)
    gates_here = mine(is_first * first_gate + is_second * second_gate)
    side_here = mine(side)
    hit = slots_here[:, :, None, :] == jnp.arange(CAP, dtype=jnp.int32)[None, None, :, None]
    pick = hit.astype(jnp.bfloat16)
    row_gate = jnp.sum(jnp.where(hit, gates_here[:, :, None, :], 0.0), axis=-1)
    row_gate = row_gate.transpose(1, 0, 2).reshape(here, blocks * CAP, 1)

    def to_slots(tokens):
        picked = jnp.einsum("nect,ntd->encd", pick, tokens, preferred_element_type=jnp.float32)
        return picked.astype(jnp.bfloat16).reshape(here, blocks * CAP, width)

    def to_tokens(slot_rows):
        return jnp.einsum(
            "nect,encd->ntd",
            pick,
            slot_rows.reshape(here, blocks, CAP, width),
            preferred_element_type=jnp.float32,
        )

    expert_rows = to_slots(rows)
    preact = jnp.einsum(
        "erd,edf->erf", expert_rows, up_weight, preferred_element_type=jnp.float32
    )
    hidden = gelu_value(preact).astype(jnp.bfloat16)
    out = jnp.einsum("erf,efd->erd", hidden, down_weight, preferred_element_type=jnp.float32)
    mixed = bring_home(to_tokens((row_gate * out).astype(jnp.bfloat16)))
    mixed_rows = (hidden_states.astype(jnp.float32) + mixed).astype(jnp.bfloat16)
    projected = jnp.dot(mixed_rows, projection, preferred_element_type=jnp.float32)
    vec_norm = jnp.sqrt(jnp.sum(projected * projected, axis=-1, keepdims=True) + norm_eps)
    vectors = projected / vec_norm
    pairs_here = teacher_scores.shape[0]
    pair_kl, vector_grad = distill(
        vectors.reshape(pairs_here, -1, projected.shape[1]),
        teacher_scores,
        query_lengths,
        passage_lengths,
    )
    vector_grad = vector_grad.reshape(tok_rows, -1)
    radial = jnp.sum(vectors * vector_grad, axis=-1, keepdims=True)
    projected_grad = ((vector_grad - vectors * radial) / vec_norm).astype(jnp.bfloat16)
    mixed_grad = jnp.dot(projected_grad, projection.T, preferred_element_type=jnp.float32)
    grad_rows = to_slots(spread_out(mixed_grad.astype(jnp.bfloat16))).astype(jnp.float32)
    out_grad = (row_gate * grad_rows).astype(jnp.bfloat16)
    product = jnp.einsum("erf,erd->efd", hidden, out_grad, preferred_element_type=jnp.float32)
    down_grad = scatter_sum(product)
    gate_grad = jnp.sum(grad_rows * out, axis=-1).reshape(here, blocks, CAP).transpose(1, 0, 2)
    hit_grad = jnp.sum(jnp.where(hit, gate_grad[..., None], 0.0), axis=2)
    spread = jnp.sum(hit_grad * side_here, axis=1, keepdims=True) * first_gate * second_gate
    router_part = jnp.einsum(
        "net,de->ntd",
        spread * side,
        router_weight.astype(jnp.float32),
        precision=lax.Precision.HIGHEST,
    )
    hidden_grad = jnp.einsum(
        "erd,efd->erf", out_grad, down_weight, preferred_element_type=jnp.float32
    )
    pre_grad = (hidden_grad * gelu_slope(preact)).astype(jnp.bfloat16)
    row_grad = jnp.einsum(
        "erf,edf->erd", pre_grad, up_weight, preferred_element_type=jnp.float32
    ).astype(jnp.bfloat16)
    input_grad = (mixed_grad + bring_home(to_tokens(row_grad) + router_part)).astype(jnp.bfloat16)
    return (input_grad, down_grad, pair_kl)


def solution(mesh):
    placed = (
        P(("rep", "exp"), None),
        P(("rep", "exp"), None),
        P(),
        P("exp", None, None),
        P("exp", None, None),
        P(),
        P(("rep", "exp"), None, None),
        P(("rep", "exp")),
        P(("rep", "exp")),
    )
    return jax.shard_map(
        local,
        mesh=mesh,
        in_specs=placed,
        out_specs=(P(("rep", "exp"), None), P("exp", "rep", None), P(("rep", "exp"))),
        check_vma=False,
    )
```

```python
import jax
import jax.numpy as jnp
from jax import lax
from jax.sharding import PartitionSpec as P

E = 8
LQ = 32
LP = 224
CAP = 96


score_scale = 20.0
norm_eps = 1e-06
sqrt_half = 0.7071067811865476
density_scale = 0.3989422804014327


def gelu_value(preact):
    return 0.5 * preact * (1.0 + lax.erf(preact * sqrt_half))


def gelu_slope(preact):
    return (
        0.5 * (1.0 + lax.erf(preact * sqrt_half))
        + preact * jnp.exp(-0.5 * preact * preact) * density_scale
    )


def distill(vectors, teacher_scores, query_lengths, passage_lengths):
    queries = vectors[:, :LQ]
    passages = vectors[:, LQ:]
    scores = score_scale * jnp.einsum(
        "pqv,pkv->pqk", queries, passages, precision=lax.Precision.HIGHEST
    )
    query_mask = (jnp.arange(LQ, dtype=jnp.int32)[None, :] < query_lengths[:, None]).astype(
        jnp.float32
    )
    passage_mask = (jnp.arange(LP, dtype=jnp.int32)[None, :] < passage_lengths[:, None]).astype(
        jnp.float32
    )
    student_exp = jnp.exp(scores) * passage_mask[:, None, :]
    student_total = jnp.sum(student_exp, axis=-1, keepdims=True)
    student = student_exp / student_total
    log_student = scores - jnp.log(student_total)
    teacher_exp = jnp.exp(teacher_scores) * passage_mask[:, None, :]
    teacher_total = jnp.sum(teacher_exp, axis=-1, keepdims=True)
    teacher = teacher_exp / teacher_total
    log_teacher = teacher_scores - jnp.log(teacher_total)
    per_query = jnp.sum(teacher * (log_teacher - log_student), axis=-1)
    pair_kl = jnp.sum(per_query * query_mask, axis=-1)
    score_grad = (student - teacher) * query_mask[:, :, None]
    query_grad = score_scale * jnp.einsum(
        "pqk,pkv->pqv", score_grad, passages, precision=lax.Precision.HIGHEST
    )
    passage_grad = score_scale * jnp.einsum(
        "pqk,pqv->pkv", score_grad, queries, precision=lax.Precision.HIGHEST
    )
    return (pair_kl, jnp.concatenate([query_grad, passage_grad], axis=1))


def fetch(block, shift):
    size = lax.axis_size("exp")
    return lax.ppermute(block, "exp", [(i, (i - shift) % size) for i in range(size)])


def give_back(block, shift):
    size = lax.axis_size("exp")
    return lax.ppermute(block, "exp", [(i, (i + shift) % size) for i in range(size)])


def spread_out(block):
    size = lax.axis_size("exp")
    return jnp.stack([block] + [fetch(block, shift) for shift in range(1, size)])


def bring_home(parts):
    total = parts[0]
    for shift in range(1, parts.shape[0]):
        total = total + give_back(parts[shift].astype(jnp.bfloat16), shift).astype(jnp.float32)
    return total


def halving_orders(bits, experts):
    near = list(range(bits))
    late = [0] + list(range(2, bits)) + [1] if bits > 2 else near
    return [late if expert % 4 == 3 else near for expert in range(experts)]


def weight_grad(hidden, out_grad):
    size = lax.axis_size("rep")
    bits = size.bit_length() - 1
    experts, rows, units = hidden.shape
    share = units // size
    index = lax.axis_index("rep")
    split = hidden.reshape(experts, rows, size // 2, 2, share)
    core = index % 2

    def product(expert, side):
        part = lax.dynamic_index_in_dim(split[expert], side, axis=2, keepdims=False)
        return jnp.einsum(
            "rf,rd->fd",
            part.reshape(rows, units // 2),
            out_grad[expert],
            preferred_element_type=jnp.float32,
        )

    def swap(block, bit):
        return lax.ppermute(block, "rep", [(i, i ^ (1 << bit)) for i in range(size)])

    orders = halving_orders(bits, experts)
    arriving = [swap(product(e, 1 - core).astype(jnp.bfloat16), 0) for e in range(experts)]
    kept = [product(e, core) for e in range(experts)]
    left = [list(range(bits - 1, 0, -1)) for _ in range(experts)]
    for step in range(1, bits):
        for e in range(experts):
            bit = orders[e][step]
            axis = left[e].index(bit)
            shape = (2,) * len(left[e]) + (share, out_grad.shape[-1])
            here = (index >> bit) % 2
            pick = lambda value, side: lax.dynamic_index_in_dim(
                value.reshape(shape), side, axis=axis, keepdims=False
            )
            sent = pick(kept[e], 1 - here).astype(jnp.float32) + pick(arriving[e], 1 - here).astype(
                jnp.float32
            )
            kept[e] = pick(kept[e], here).astype(jnp.float32) + pick(arriving[e], here).astype(
                jnp.float32
            )
            arriving[e] = swap(sent.astype(jnp.bfloat16), bit)
            left[e].remove(bit)
    return jnp.stack(
        [(kept[e] + arriving[e].astype(jnp.float32)).reshape(share, -1) for e in range(experts)]
    )


def local(
    hidden_states,
    expert_ids,
    router_weight,
    up_weight,
    down_weight,
    projection,
    teacher_scores,
    query_lengths,
    passage_lengths,
):
    tok_rows, width = hidden_states.shape
    here = up_weight.shape[0]
    first = lax.axis_index("exp") * here
    rows = spread_out(hidden_states)
    ids = spread_out(expert_ids.T)
    blocks = rows.shape[0]
    names = jnp.arange(E, dtype=jnp.int32)[None, :, None]
    is_first = (ids[:, :1] == names).astype(jnp.float32)
    is_second = (ids[:, 1:] == names).astype(jnp.float32)
    logits = jnp.einsum("de,ntd->net", router_weight, rows, preferred_element_type=jnp.float32)
    side = is_first - is_second
    first_gate = jax.nn.sigmoid(jnp.sum(logits * side, axis=1, keepdims=True))
    second_gate = 1.0 - first_gate
    named = is_first + is_second
    before = jnp.arange(tok_rows)[:, None] < jnp.arange(tok_rows)[None, :]
    slots = jnp.einsum(
        "net,tu->neu",
        named.astype(jnp.bfloat16),
        before.astype(jnp.bfloat16),
        preferred_element_type=jnp.float32,
    ).astype(jnp.int32)
    slots = jnp.where(named > 0, slots, -1)
    mine = lambda value: lax.dynamic_slice_in_dim(value, first, here, axis=1)
    slots_here = mine(slots)
    gates_here = mine(is_first * first_gate + is_second * second_gate)
    side_here = mine(side)
    hit = slots_here[:, :, None, :] == jnp.arange(CAP, dtype=jnp.int32)[None, None, :, None]
    pick = hit.astype(jnp.bfloat16)
    row_gate = jnp.sum(jnp.where(hit, gates_here[:, :, None, :], 0.0), axis=-1)
    row_gate = row_gate.transpose(1, 0, 2).reshape(here, blocks * CAP, 1)

    def to_slots(tokens):
        picked = jnp.einsum("nect,ntd->encd", pick, tokens, preferred_element_type=jnp.float32)
        return picked.astype(jnp.bfloat16).reshape(here, blocks * CAP, width)

    def to_tokens(slot_rows):
        return jnp.einsum(
            "nect,encd->ntd",
            pick,
            slot_rows.reshape(here, blocks, CAP, width),
            preferred_element_type=jnp.float32,
        )

    expert_rows = to_slots(rows)
    preact = jnp.einsum(
        "erd,edf->erf", expert_rows, up_weight, preferred_element_type=jnp.float32
    )
    hidden = gelu_value(preact).astype(jnp.bfloat16)
    out = jnp.einsum("erf,efd->erd", hidden, down_weight, preferred_element_type=jnp.float32)
    mixed = bring_home(to_tokens((row_gate * out).astype(jnp.bfloat16)))
    mixed_rows = (hidden_states.astype(jnp.float32) + mixed).astype(jnp.bfloat16)
    projected = jnp.dot(mixed_rows, projection, preferred_element_type=jnp.float32)
    vec_norm = jnp.sqrt(jnp.sum(projected * projected, axis=-1, keepdims=True) + norm_eps)
    vectors = projected / vec_norm
    pairs_here = teacher_scores.shape[0]
    pair_kl, vector_grad = distill(
        vectors.reshape(pairs_here, -1, projected.shape[1]),
        teacher_scores,
        query_lengths,
        passage_lengths,
    )
    vector_grad = vector_grad.reshape(tok_rows, -1)
    radial = jnp.sum(vectors * vector_grad, axis=-1, keepdims=True)
    projected_grad = ((vector_grad - vectors * radial) / vec_norm).astype(jnp.bfloat16)
    mixed_grad = jnp.dot(projected_grad, projection.T, preferred_element_type=jnp.float32)
    grad_rows = to_slots(spread_out(mixed_grad.astype(jnp.bfloat16))).astype(jnp.float32)
    out_grad = (row_gate * grad_rows).astype(jnp.bfloat16)
    down_grad = weight_grad(hidden, out_grad)
    gate_grad = jnp.sum(grad_rows * out, axis=-1).reshape(here, blocks, CAP).transpose(1, 0, 2)
    hit_grad = jnp.sum(jnp.where(hit, gate_grad[..., None], 0.0), axis=2)
    spread = jnp.sum(hit_grad * side_here, axis=1, keepdims=True) * first_gate * second_gate
    router_part = jnp.einsum(
        "net,de->ntd",
        spread * side,
        router_weight.astype(jnp.float32),
        precision=lax.Precision.HIGHEST,
    )
    hidden_grad = jnp.einsum(
        "erd,efd->erf", out_grad, down_weight, preferred_element_type=jnp.float32
    )
    pre_grad = (hidden_grad * gelu_slope(preact)).astype(jnp.bfloat16)
    row_grad = jnp.einsum(
        "erf,edf->erd", pre_grad, up_weight, preferred_element_type=jnp.float32
    ).astype(jnp.bfloat16)
    input_grad = (mixed_grad + bring_home(to_tokens(row_grad) + router_part)).astype(jnp.bfloat16)
    return (input_grad, down_grad, pair_kl)


def solution(mesh):
    placed = (
        P(("rep", "exp"), None),
        P(("rep", "exp"), None),
        P(),
        P("exp", None, None),
        P("exp", None, None),
        P(),
        P(("rep", "exp"), None, None),
        P(("rep", "exp")),
        P(("rep", "exp")),
    )
    return jax.shard_map(
        local,
        mesh=mesh,
        in_specs=placed,
        out_specs=(P(("rep", "exp"), None), P("exp", "rep", None), P(("rep", "exp"))),
        check_vma=False,
    )
```

```python
import jax
import jax.numpy as jnp
from jax import lax
from jax.sharding import PartitionSpec as P

E = 8
LQ = 32
LP = 224
CAP = 96


score_scale = 20.0
norm_eps = 1e-06
sqrt_half = 0.7071067811865476
density_scale = 0.3989422804014327


def gelu_value(preact):
    return 0.5 * preact * (1.0 + lax.erf(preact * sqrt_half))


def gelu_slope(preact):
    return (
        0.5 * (1.0 + lax.erf(preact * sqrt_half))
        + preact * jnp.exp(-0.5 * preact * preact) * density_scale
    )


def distill(vectors, teacher_scores, query_lengths, passage_lengths):
    queries = vectors[:, :LQ]
    passages = vectors[:, LQ:]
    scores = score_scale * jnp.einsum(
        "pqv,pkv->pqk", queries, passages, precision=lax.Precision.HIGHEST
    )
    query_mask = (jnp.arange(LQ, dtype=jnp.int32)[None, :] < query_lengths[:, None]).astype(
        jnp.float32
    )
    passage_mask = (jnp.arange(LP, dtype=jnp.int32)[None, :] < passage_lengths[:, None]).astype(
        jnp.float32
    )
    student_exp = jnp.exp(scores) * passage_mask[:, None, :]
    student_total = jnp.sum(student_exp, axis=-1, keepdims=True)
    student = student_exp / student_total
    log_student = scores - jnp.log(student_total)
    teacher_exp = jnp.exp(teacher_scores) * passage_mask[:, None, :]
    teacher_total = jnp.sum(teacher_exp, axis=-1, keepdims=True)
    teacher = teacher_exp / teacher_total
    log_teacher = teacher_scores - jnp.log(teacher_total)
    per_query = jnp.sum(teacher * (log_teacher - log_student), axis=-1)
    pair_kl = jnp.sum(per_query * query_mask, axis=-1)
    score_grad = (student - teacher) * query_mask[:, :, None]
    query_grad = score_scale * jnp.einsum(
        "pqk,pkv->pqv", score_grad, passages, precision=lax.Precision.HIGHEST
    )
    passage_grad = score_scale * jnp.einsum(
        "pqk,pqv->pkv", score_grad, queries, precision=lax.Precision.HIGHEST
    )
    return (pair_kl, jnp.concatenate([query_grad, passage_grad], axis=1))


def fetch(block, shift):
    size = lax.axis_size("exp")
    return lax.ppermute(block, "exp", [(i, (i - shift) % size) for i in range(size)])


def give_back(block, shift):
    size = lax.axis_size("exp")
    return lax.ppermute(block, "exp", [(i, (i + shift) % size) for i in range(size)])


def spread_out(block):
    size = lax.axis_size("exp")
    return jnp.stack([block] + [fetch(block, shift) for shift in range(1, size)])


def bring_home(parts):
    total = parts[0]
    for shift in range(1, parts.shape[0]):
        total = total + give_back(parts[shift].astype(jnp.bfloat16), shift).astype(jnp.float32)
    return total


def halving_orders(bits, experts):
    near = list(range(bits))
    late = [0] + list(range(2, bits)) + [1] if bits > 2 else near
    return [late if expert % 4 == 3 else near for expert in range(experts)]


def weight_grad(hidden, out_grad):
    size = lax.axis_size("rep")
    bits = size.bit_length() - 1
    experts, _, units = hidden.shape
    width = out_grad.shape[-1]
    share = units // size
    index = lax.axis_index("rep")
    product = jnp.einsum(
        "erf,erd->efd", hidden, out_grad, preferred_element_type=jnp.float32
    ).astype(jnp.bfloat16)

    def swap(block, bit):
        return lax.ppermute(block, "rep", [(i, i ^ (1 << bit)) for i in range(size)])

    orders = halving_orders(bits, experts)
    left = [list(range(bits - 1, -1, -1)) for _ in range(experts)]
    held = [[product[e]] for e in range(experts)]
    for step in range(bits):
        sent = []
        for e in range(experts):
            bit = orders[e][step]
            axis = left[e].index(bit)
            shape = (2,) * len(left[e]) + (share, width)
            here = (index >> bit) % 2

            def half(side):
                total = None
                for term in held[e]:
                    piece = lax.dynamic_index_in_dim(
                        term.reshape(shape), side, axis=axis, keepdims=False
                    ).astype(jnp.float32)
                    total = piece if total is None else total + piece
                return total

            sent.append(half(1 - here).astype(jnp.bfloat16))
            held[e] = [half(here)]
            left[e].remove(bit)
        for e in range(experts):
            held[e].append(swap(sent[e], orders[e][step]))
        if step == min(1, bits - 1):
            held[0], out_grad = lax.optimization_barrier((held[0], out_grad))
    shares = [
        sum(term.astype(jnp.float32).reshape(share, width) for term in held[e])
        for e in range(experts)
    ]
    return jnp.stack(shares), out_grad


def local(
    hidden_states,
    expert_ids,
    router_weight,
    up_weight,
    down_weight,
    projection,
    teacher_scores,
    query_lengths,
    passage_lengths,
):
    tok_rows, width = hidden_states.shape
    here = up_weight.shape[0]
    first = lax.axis_index("exp") * here
    rows = spread_out(hidden_states)
    ids = spread_out(expert_ids.T)
    blocks = rows.shape[0]
    names = jnp.arange(E, dtype=jnp.int32)[None, :, None]
    is_first = (ids[:, :1] == names).astype(jnp.float32)
    is_second = (ids[:, 1:] == names).astype(jnp.float32)
    logits = jnp.einsum("de,ntd->net", router_weight, rows, preferred_element_type=jnp.float32)
    side = is_first - is_second
    first_gate = jax.nn.sigmoid(jnp.sum(logits * side, axis=1, keepdims=True))
    second_gate = 1.0 - first_gate
    named = is_first + is_second
    before = jnp.arange(tok_rows)[:, None] < jnp.arange(tok_rows)[None, :]
    slots = jnp.einsum(
        "net,tu->neu",
        named.astype(jnp.bfloat16),
        before.astype(jnp.bfloat16),
        preferred_element_type=jnp.float32,
    ).astype(jnp.int32)
    slots = jnp.where(named > 0, slots, -1)
    mine = lambda value: lax.dynamic_slice_in_dim(value, first, here, axis=1)
    slots_here = mine(slots)
    gates_here = mine(is_first * first_gate + is_second * second_gate)
    side_here = mine(side)
    hit = slots_here[:, :, None, :] == jnp.arange(CAP, dtype=jnp.int32)[None, None, :, None]
    pick = hit.astype(jnp.bfloat16)
    row_gate = jnp.sum(jnp.where(hit, gates_here[:, :, None, :], 0.0), axis=-1)
    row_gate = row_gate.transpose(1, 0, 2).reshape(here, blocks * CAP, 1)

    def to_slots(tokens):
        picked = jnp.einsum("nect,ntd->encd", pick, tokens, preferred_element_type=jnp.float32)
        return picked.astype(jnp.bfloat16).reshape(here, blocks * CAP, width)

    def to_tokens(slot_rows):
        return jnp.einsum(
            "nect,encd->ntd",
            pick,
            slot_rows.reshape(here, blocks, CAP, width),
            preferred_element_type=jnp.float32,
        )

    expert_rows = to_slots(rows)
    preact = jnp.einsum(
        "erd,edf->erf", expert_rows, up_weight, preferred_element_type=jnp.float32
    )
    hidden = gelu_value(preact).astype(jnp.bfloat16)
    out = jnp.einsum("erf,efd->erd", hidden, down_weight, preferred_element_type=jnp.float32)
    mixed = bring_home(to_tokens((row_gate * out).astype(jnp.bfloat16)))
    mixed_rows = (hidden_states.astype(jnp.float32) + mixed).astype(jnp.bfloat16)
    projected = jnp.dot(mixed_rows, projection, preferred_element_type=jnp.float32)
    vec_norm = jnp.sqrt(jnp.sum(projected * projected, axis=-1, keepdims=True) + norm_eps)
    vectors = projected / vec_norm
    pairs_here = teacher_scores.shape[0]
    pair_kl, vector_grad = distill(
        vectors.reshape(pairs_here, -1, projected.shape[1]),
        teacher_scores,
        query_lengths,
        passage_lengths,
    )
    vector_grad = vector_grad.reshape(tok_rows, -1)
    radial = jnp.sum(vectors * vector_grad, axis=-1, keepdims=True)
    projected_grad = ((vector_grad - vectors * radial) / vec_norm).astype(jnp.bfloat16)
    mixed_grad = jnp.dot(projected_grad, projection.T, preferred_element_type=jnp.float32)
    grad_rows = to_slots(spread_out(mixed_grad.astype(jnp.bfloat16))).astype(jnp.float32)
    out_grad = (row_gate * grad_rows).astype(jnp.bfloat16)
    down_grad, out_grad = weight_grad(hidden, out_grad)
    gate_grad = jnp.sum(grad_rows * out, axis=-1).reshape(here, blocks, CAP).transpose(1, 0, 2)
    hit_grad = jnp.sum(jnp.where(hit, gate_grad[..., None], 0.0), axis=2)
    spread = jnp.sum(hit_grad * side_here, axis=1, keepdims=True) * first_gate * second_gate
    router_part = jnp.einsum(
        "net,de->ntd",
        spread * side,
        router_weight.astype(jnp.float32),
        precision=lax.Precision.HIGHEST,
    )
    hidden_grad = jnp.einsum(
        "erd,efd->erf", out_grad, down_weight, preferred_element_type=jnp.float32
    )
    pre_grad = (hidden_grad * gelu_slope(preact)).astype(jnp.bfloat16)
    row_grad = jnp.einsum(
        "erf,edf->erd", pre_grad, up_weight, preferred_element_type=jnp.float32
    ).astype(jnp.bfloat16)
    input_grad = (mixed_grad + bring_home(to_tokens(row_grad) + router_part)).astype(jnp.bfloat16)
    return (input_grad, down_grad, pair_kl)


def solution(mesh):
    placed = (
        P(("rep", "exp"), None),
        P(("rep", "exp"), None),
        P(),
        P("exp", None, None),
        P("exp", None, None),
        P(),
        P(("rep", "exp"), None, None),
        P(("rep", "exp")),
        P(("rep", "exp")),
    )
    return jax.shard_map(
        local,
        mesh=mesh,
        in_specs=placed,
        out_specs=(P(("rep", "exp"), None), P("exp", "rep", None), P(("rep", "exp"))),
        check_vma=False,
    )
```

```python
import jax
import jax.numpy as jnp
from jax import lax
from jax.sharding import PartitionSpec as P

E = 8
LQ = 32
LP = 224
CAP = 96


score_scale = 20.0
norm_eps = 1e-06
sqrt_half = 0.7071067811865476
density_scale = 0.3989422804014327


def gelu_value(preact):
    return 0.5 * preact * (1.0 + lax.erf(preact * sqrt_half))


def gelu_slope(preact):
    return (
        0.5 * (1.0 + lax.erf(preact * sqrt_half))
        + preact * jnp.exp(-0.5 * preact * preact) * density_scale
    )


def distill(vectors, teacher_scores, query_lengths, passage_lengths):
    queries = vectors[:, :LQ]
    passages = vectors[:, LQ:]
    scores = score_scale * jnp.einsum(
        "pqv,pkv->pqk", queries, passages, precision=lax.Precision.HIGHEST
    )
    query_mask = (jnp.arange(LQ, dtype=jnp.int32)[None, :] < query_lengths[:, None]).astype(
        jnp.float32
    )
    passage_mask = (jnp.arange(LP, dtype=jnp.int32)[None, :] < passage_lengths[:, None]).astype(
        jnp.float32
    )
    student_exp = jnp.exp(scores) * passage_mask[:, None, :]
    student_total = jnp.sum(student_exp, axis=-1, keepdims=True)
    student = student_exp / student_total
    log_student = scores - jnp.log(student_total)
    teacher_exp = jnp.exp(teacher_scores) * passage_mask[:, None, :]
    teacher_total = jnp.sum(teacher_exp, axis=-1, keepdims=True)
    teacher = teacher_exp / teacher_total
    log_teacher = teacher_scores - jnp.log(teacher_total)
    per_query = jnp.sum(teacher * (log_teacher - log_student), axis=-1)
    pair_kl = jnp.sum(per_query * query_mask, axis=-1)
    score_grad = (student - teacher) * query_mask[:, :, None]
    query_grad = score_scale * jnp.einsum(
        "pqk,pkv->pqv", score_grad, passages, precision=lax.Precision.HIGHEST
    )
    passage_grad = score_scale * jnp.einsum(
        "pqk,pqv->pkv", score_grad, queries, precision=lax.Precision.HIGHEST
    )
    return (pair_kl, jnp.concatenate([query_grad, passage_grad], axis=1))


def fetch(block, shift):
    size = lax.axis_size("exp")
    return lax.ppermute(block, "exp", [(i, (i - shift) % size) for i in range(size)])


def give_back(block, shift):
    size = lax.axis_size("exp")
    return lax.ppermute(block, "exp", [(i, (i + shift) % size) for i in range(size)])


def spread_out(block):
    size = lax.axis_size("exp")
    return jnp.stack([block] + [fetch(block, shift) for shift in range(1, size)])


def bring_home(parts):
    total = parts[0]
    for shift in range(1, parts.shape[0]):
        total = total + give_back(parts[shift].astype(jnp.bfloat16), shift).astype(jnp.float32)
    return total


def weight_grad(hidden, out_grad):
    size = lax.axis_size("rep")
    bits = size.bit_length() - 1
    experts, _, units = hidden.shape
    width = out_grad.shape[-1]
    share = units // size
    index = lax.axis_index("rep")
    product = jnp.einsum(
        "erf,erd->efd", hidden, out_grad, preferred_element_type=jnp.float32
    ).astype(jnp.bfloat16)

    def swap(block, bit):
        return lax.ppermute(block, "rep", [(i, i ^ (1 << bit)) for i in range(size)])

    def cut(terms, left, bit, side):
        shape = (-1,) + (2,) * len(left) + (share, width)
        axis = 1 + left.index(bit)
        pieces = [
            lax.dynamic_index_in_dim(term.reshape(shape), side, axis=axis, keepdims=False)
            for term in terms
        ]
        if len(pieces) == 1:
            return pieces[0]
        return sum(piece.astype(jnp.float32) for piece in pieces)

    def step(terms, left, bit):
        here = (index >> bit) % 2
        sent = cut(terms, left, bit, 1 - here).astype(jnp.bfloat16)
        return [cut(terms, left, bit, here), swap(sent, bit)], [b for b in left if b != bit]

    held, left = step([product], list(range(bits - 1, -1, -1)), 0)
    group = max(1, experts // 2)
    orders = [list(range(1, bits)), list(range(2, bits)) + [1]]
    chains = [
        ([term[start : start + group] for term in held], left)
        for start in range(0, experts, group)
    ]
    for number in range(bits - 1):
        chains = [step(*chain, orders[at % 2][number]) for at, chain in enumerate(chains)]
    shares = [
        sum(term.astype(jnp.float32).reshape(-1, share, width) for term in terms)
        for terms, _ in chains
    ]
    return jnp.concatenate(shares)


def local(
    hidden_states,
    expert_ids,
    router_weight,
    up_weight,
    down_weight,
    projection,
    teacher_scores,
    query_lengths,
    passage_lengths,
):
    tok_rows, width = hidden_states.shape
    here = up_weight.shape[0]
    first = lax.axis_index("exp") * here
    rows = spread_out(hidden_states)
    ids = spread_out(expert_ids.T)
    blocks = rows.shape[0]
    names = jnp.arange(E, dtype=jnp.int32)[None, :, None]
    is_first = (ids[:, :1] == names).astype(jnp.float32)
    is_second = (ids[:, 1:] == names).astype(jnp.float32)
    logits = jnp.einsum("de,ntd->net", router_weight, rows, preferred_element_type=jnp.float32)
    side = is_first - is_second
    first_gate = jax.nn.sigmoid(jnp.sum(logits * side, axis=1, keepdims=True))
    second_gate = 1.0 - first_gate
    named = is_first + is_second
    before = jnp.arange(tok_rows)[:, None] < jnp.arange(tok_rows)[None, :]
    slots = jnp.einsum(
        "net,tu->neu",
        named.astype(jnp.bfloat16),
        before.astype(jnp.bfloat16),
        preferred_element_type=jnp.float32,
    ).astype(jnp.int32)
    slots = jnp.where(named > 0, slots, -1)
    mine = lambda value: lax.dynamic_slice_in_dim(value, first, here, axis=1)
    slots_here = mine(slots)
    gates_here = mine(is_first * first_gate + is_second * second_gate)
    side_here = mine(side)
    hit = slots_here[:, :, None, :] == jnp.arange(CAP, dtype=jnp.int32)[None, None, :, None]
    pick = hit.astype(jnp.bfloat16)
    row_gate = jnp.sum(jnp.where(hit, gates_here[:, :, None, :], 0.0), axis=-1)
    row_gate = row_gate.transpose(1, 0, 2).reshape(here, blocks * CAP, 1)

    def to_slots(tokens):
        picked = jnp.einsum("nect,ntd->encd", pick, tokens, preferred_element_type=jnp.float32)
        return picked.astype(jnp.bfloat16).reshape(here, blocks * CAP, width)

    def to_tokens(slot_rows):
        return jnp.einsum(
            "nect,encd->ntd",
            pick,
            slot_rows.reshape(here, blocks, CAP, width),
            preferred_element_type=jnp.float32,
        )

    expert_rows = to_slots(rows)
    preact = jnp.einsum(
        "erd,edf->erf", expert_rows, up_weight, preferred_element_type=jnp.float32
    )
    hidden = gelu_value(preact).astype(jnp.bfloat16)
    out = jnp.einsum("erf,efd->erd", hidden, down_weight, preferred_element_type=jnp.float32)
    mixed = bring_home(to_tokens((row_gate * out).astype(jnp.bfloat16)))
    mixed_rows = (hidden_states.astype(jnp.float32) + mixed).astype(jnp.bfloat16)
    projected = jnp.dot(mixed_rows, projection, preferred_element_type=jnp.float32)
    vec_norm = jnp.sqrt(jnp.sum(projected * projected, axis=-1, keepdims=True) + norm_eps)
    vectors = projected / vec_norm
    pairs_here = teacher_scores.shape[0]
    pair_kl, vector_grad = distill(
        vectors.reshape(pairs_here, -1, projected.shape[1]),
        teacher_scores,
        query_lengths,
        passage_lengths,
    )
    vector_grad = vector_grad.reshape(tok_rows, -1)
    radial = jnp.sum(vectors * vector_grad, axis=-1, keepdims=True)
    projected_grad = ((vector_grad - vectors * radial) / vec_norm).astype(jnp.bfloat16)
    mixed_grad = jnp.dot(projected_grad, projection.T, preferred_element_type=jnp.float32)
    grad_rows = to_slots(spread_out(mixed_grad.astype(jnp.bfloat16))).astype(jnp.float32)
    out_grad = (row_gate * grad_rows).astype(jnp.bfloat16)
    down_grad = weight_grad(hidden, out_grad)
    gate_grad = jnp.sum(grad_rows * out, axis=-1).reshape(here, blocks, CAP).transpose(1, 0, 2)
    hit_grad = jnp.sum(jnp.where(hit, gate_grad[..., None], 0.0), axis=2)
    spread = jnp.sum(hit_grad * side_here, axis=1, keepdims=True) * first_gate * second_gate
    router_part = jnp.einsum(
        "net,de->ntd",
        spread * side,
        router_weight.astype(jnp.float32),
        precision=lax.Precision.HIGHEST,
    )
    hidden_grad = jnp.einsum(
        "erd,efd->erf", out_grad, down_weight, preferred_element_type=jnp.float32
    )
    pre_grad = (hidden_grad * gelu_slope(preact)).astype(jnp.bfloat16)
    row_grad = jnp.einsum(
        "erf,edf->erd", pre_grad, up_weight, preferred_element_type=jnp.float32
    ).astype(jnp.bfloat16)
    input_grad = (mixed_grad + bring_home(to_tokens(row_grad) + router_part)).astype(jnp.bfloat16)
    return (input_grad, down_grad, pair_kl)


def solution(mesh):
    placed = (
        P(("rep", "exp"), None),
        P(("rep", "exp"), None),
        P(),
        P("exp", None, None),
        P("exp", None, None),
        P(),
        P(("rep", "exp"), None, None),
        P(("rep", "exp")),
        P(("rep", "exp")),
    )
    return jax.shard_map(
        local,
        mesh=mesh,
        in_specs=placed,
        out_specs=(P(("rep", "exp"), None), P("exp", "rep", None), P(("rep", "exp"))),
        check_vma=False,
    )
```

```python
import jax
import jax.numpy as jnp
from jax import lax
from jax.sharding import PartitionSpec as P

E = 8
LQ = 32
LP = 224
CAP = 96


score_scale = 20.0
norm_eps = 1e-06
sqrt_half = 0.7071067811865476
density_scale = 0.3989422804014327


def gelu_value(preact):
    return 0.5 * preact * (1.0 + lax.erf(preact * sqrt_half))


def gelu_slope(preact):
    return (
        0.5 * (1.0 + lax.erf(preact * sqrt_half))
        + preact * jnp.exp(-0.5 * preact * preact) * density_scale
    )


def distill(vectors, teacher_scores, query_lengths, passage_lengths):
    queries = vectors[:, :LQ]
    passages = vectors[:, LQ:]
    scores = score_scale * jnp.einsum(
        "pqv,pkv->pqk", queries, passages, precision=lax.Precision.HIGHEST
    )
    query_mask = (jnp.arange(LQ, dtype=jnp.int32)[None, :] < query_lengths[:, None]).astype(
        jnp.float32
    )
    passage_mask = (jnp.arange(LP, dtype=jnp.int32)[None, :] < passage_lengths[:, None]).astype(
        jnp.float32
    )
    student_exp = jnp.exp(scores) * passage_mask[:, None, :]
    student_total = jnp.sum(student_exp, axis=-1, keepdims=True)
    student = student_exp / student_total
    log_student = scores - jnp.log(student_total)
    teacher_exp = jnp.exp(teacher_scores) * passage_mask[:, None, :]
    teacher_total = jnp.sum(teacher_exp, axis=-1, keepdims=True)
    teacher = teacher_exp / teacher_total
    log_teacher = teacher_scores - jnp.log(teacher_total)
    per_query = jnp.sum(teacher * (log_teacher - log_student), axis=-1)
    pair_kl = jnp.sum(per_query * query_mask, axis=-1)
    score_grad = (student - teacher) * query_mask[:, :, None]
    query_grad = score_scale * jnp.einsum(
        "pqk,pkv->pqv", score_grad, passages, precision=lax.Precision.HIGHEST
    )
    passage_grad = score_scale * jnp.einsum(
        "pqk,pqv->pkv", score_grad, queries, precision=lax.Precision.HIGHEST
    )
    return (pair_kl, jnp.concatenate([query_grad, passage_grad], axis=1))


def fetch(block, shift):
    size = lax.axis_size("exp")
    return lax.ppermute(block, "exp", [(i, (i - shift) % size) for i in range(size)])


def give_back(block, shift):
    size = lax.axis_size("exp")
    return lax.ppermute(block, "exp", [(i, (i + shift) % size) for i in range(size)])


def spread_out(block):
    size = lax.axis_size("exp")
    return jnp.stack([block] + [fetch(block, shift) for shift in range(1, size)])


def bring_home(parts):
    total = parts[0]
    for shift in range(1, parts.shape[0]):
        total = total + give_back(parts[shift].astype(jnp.bfloat16), shift).astype(jnp.float32)
    return total


def halving_orders(bits, experts):
    near = list(range(bits))
    late = [0] + list(range(2, bits)) + [1] if bits > 2 else near
    return [late if expert % 4 == 3 else near for expert in range(experts)]


def weight_grad(hidden, out_grad):
    size = lax.axis_size("rep")
    bits = size.bit_length() - 1
    experts, _, units = hidden.shape
    width = out_grad.shape[-1]
    share = units // size
    index = lax.axis_index("rep")
    product = jnp.einsum(
        "erf,erd->efd", hidden, out_grad, preferred_element_type=jnp.float32
    ).astype(jnp.bfloat16)

    def swap(block, bit):
        return lax.ppermute(block, "rep", [(i, i ^ (1 << bit)) for i in range(size)])

    orders = halving_orders(bits, experts)
    left = [list(range(bits - 1, -1, -1)) for _ in range(experts)]
    held = [[product[e]] for e in range(experts)]
    for step in range(bits):
        sent = []
        for e in range(experts):
            bit = orders[e][step]
            axis = left[e].index(bit)
            shape = (2,) * len(left[e]) + (share, width)
            here = (index >> bit) % 2

            def half(side):
                total = None
                for term in held[e]:
                    piece = lax.dynamic_index_in_dim(
                        term.reshape(shape), side, axis=axis, keepdims=False
                    ).astype(jnp.float32)
                    total = piece if total is None else total + piece
                return total

            sent.append(half(1 - here).astype(jnp.bfloat16))
            held[e] = [half(here)]
            left[e].remove(bit)
        for e in range(experts):
            held[e].append(swap(sent[e], orders[e][step]))
        if step == min(1, bits - 1):
            held[-1], out_grad = lax.optimization_barrier((held[-1], out_grad))
    shares = [
        sum(term.astype(jnp.float32).reshape(share, width) for term in held[e])
        for e in range(experts)
    ]
    return jnp.stack(shares), out_grad


def local(
    hidden_states,
    expert_ids,
    router_weight,
    up_weight,
    down_weight,
    projection,
    teacher_scores,
    query_lengths,
    passage_lengths,
):
    tok_rows, width = hidden_states.shape
    here = up_weight.shape[0]
    first = lax.axis_index("exp") * here
    rows = spread_out(hidden_states)
    ids = spread_out(expert_ids.T)
    blocks = rows.shape[0]
    names = jnp.arange(E, dtype=jnp.int32)[None, :, None]
    is_first = (ids[:, :1] == names).astype(jnp.float32)
    is_second = (ids[:, 1:] == names).astype(jnp.float32)
    logits = jnp.einsum("de,ntd->net", router_weight, rows, preferred_element_type=jnp.float32)
    side = is_first - is_second
    first_gate = jax.nn.sigmoid(jnp.sum(logits * side, axis=1, keepdims=True))
    second_gate = 1.0 - first_gate
    named = is_first + is_second
    before = jnp.arange(tok_rows)[:, None] < jnp.arange(tok_rows)[None, :]
    slots = jnp.einsum(
        "net,tu->neu",
        named.astype(jnp.bfloat16),
        before.astype(jnp.bfloat16),
        preferred_element_type=jnp.float32,
    ).astype(jnp.int32)
    slots = jnp.where(named > 0, slots, -1)
    mine = lambda value: lax.dynamic_slice_in_dim(value, first, here, axis=1)
    slots_here = mine(slots)
    gates_here = mine(is_first * first_gate + is_second * second_gate)
    side_here = mine(side)
    hit = slots_here[:, :, None, :] == jnp.arange(CAP, dtype=jnp.int32)[None, None, :, None]
    pick = hit.astype(jnp.bfloat16)
    row_gate = jnp.sum(jnp.where(hit, gates_here[:, :, None, :], 0.0), axis=-1)
    row_gate = row_gate.transpose(1, 0, 2).reshape(here, blocks * CAP, 1)

    def to_slots(tokens):
        picked = jnp.einsum("nect,ntd->encd", pick, tokens, preferred_element_type=jnp.float32)
        return picked.astype(jnp.bfloat16).reshape(here, blocks * CAP, width)

    def to_tokens(slot_rows):
        return jnp.einsum(
            "nect,encd->ntd",
            pick,
            slot_rows.reshape(here, blocks, CAP, width),
            preferred_element_type=jnp.float32,
        )

    expert_rows = to_slots(rows)
    preact = jnp.einsum(
        "erd,edf->erf", expert_rows, up_weight, preferred_element_type=jnp.float32
    )
    hidden = gelu_value(preact).astype(jnp.bfloat16)
    out = jnp.einsum("erf,efd->erd", hidden, down_weight, preferred_element_type=jnp.float32)
    mixed = bring_home(to_tokens((row_gate * out).astype(jnp.bfloat16)))
    mixed_rows = (hidden_states.astype(jnp.float32) + mixed).astype(jnp.bfloat16)
    projected = jnp.dot(mixed_rows, projection, preferred_element_type=jnp.float32)
    vec_norm = jnp.sqrt(jnp.sum(projected * projected, axis=-1, keepdims=True) + norm_eps)
    vectors = projected / vec_norm
    pairs_here = teacher_scores.shape[0]
    pair_kl, vector_grad = distill(
        vectors.reshape(pairs_here, -1, projected.shape[1]),
        teacher_scores,
        query_lengths,
        passage_lengths,
    )
    vector_grad = vector_grad.reshape(tok_rows, -1)
    radial = jnp.sum(vectors * vector_grad, axis=-1, keepdims=True)
    projected_grad = ((vector_grad - vectors * radial) / vec_norm).astype(jnp.bfloat16)
    mixed_grad = jnp.dot(projected_grad, projection.T, preferred_element_type=jnp.float32)
    grad_rows = to_slots(spread_out(mixed_grad.astype(jnp.bfloat16))).astype(jnp.float32)
    out_grad = (row_gate * grad_rows).astype(jnp.bfloat16)
    down_grad, out_grad = weight_grad(hidden, out_grad)
    gate_grad = jnp.sum(grad_rows * out, axis=-1).reshape(here, blocks, CAP).transpose(1, 0, 2)
    hit_grad = jnp.sum(jnp.where(hit, gate_grad[..., None], 0.0), axis=2)
    spread = jnp.sum(hit_grad * side_here, axis=1, keepdims=True) * first_gate * second_gate
    router_part = jnp.einsum(
        "net,de->ntd",
        spread * side,
        router_weight.astype(jnp.float32),
        precision=lax.Precision.HIGHEST,
    )
    hidden_grad = jnp.einsum(
        "erd,efd->erf", out_grad, down_weight, preferred_element_type=jnp.float32
    )
    pre_grad = (hidden_grad * gelu_slope(preact)).astype(jnp.bfloat16)
    row_grad = jnp.einsum(
        "erf,edf->erd", pre_grad, up_weight, preferred_element_type=jnp.float32
    ).astype(jnp.bfloat16)
    input_grad = (mixed_grad + bring_home(to_tokens(row_grad) + router_part)).astype(jnp.bfloat16)
    return (input_grad, down_grad, pair_kl)


def solution(mesh):
    placed = (
        P(("rep", "exp"), None),
        P(("rep", "exp"), None),
        P(),
        P("exp", None, None),
        P("exp", None, None),
        P(),
        P(("rep", "exp"), None, None),
        P(("rep", "exp")),
        P(("rep", "exp")),
    )
    return jax.shard_map(
        local,
        mesh=mesh,
        in_specs=placed,
        out_specs=(P(("rep", "exp"), None), P("exp", "rep", None), P(("rep", "exp"))),
        check_vma=False,
    )
```
